32 devices in a mesh: parts: 2 (over y), dp: 8 (over z, x), fac: 2 (over core).
Axes of the slice: x: 2, y: 2, z: 4, core: 2. Of those that a mesh axis runs over, the one named last changes fastest.
Arguments:
- acts: bfloat16 [2816, 14336], P(('parts', 'dp'), 'fac'), parts along dimension 0, may hold values from -6 to 6
- grads: bfloat16 [2816, 4096], P(('parts', 'dp'), 'fac'), parts along dimension 0, may hold values from -6 to 6
- lengths: int32 [16, 4], P(('parts', 'dp')), parts along dimension 0, may hold values from 1 to 88, 176 in all within a row
- basis_a: bfloat16 [2, 7168, 14336], P('fac', 'dp'), may hold values from -0.046875 to 0.046875
- basis_g: bfloat16 [2, 2048, 4096], P('fac', 'dp'), may hold values from -0.09375 to 0.09375
- coef_a: bfloat16 [14336, 256], P(('dp', 'fac')), may hold values from -0.009765625 to 0.009765625
- coef_g: bfloat16 [4096, 256], P(('dp', 'fac')), may hold values from -0.01953125 to 0.01953125
- eig_a: float32 [14336], P(('dp', 'fac')), may hold values from 0.02 to 2
- eig_g: float32 [4096], P(('dp', 'fac')), may hold values from 0.02 to 2
Outputs:
- scores: float32 [64, 8], P(('parts', 'dp'), 'fac'), parts along dimension 0
The draws below stay inside these ranges and needn't reach their ends.
There are 2 independent parts, one for each index of `parts`. The reference program is written for one: setup_inputs(seed, part) draws one part's arguments, and reference() takes and returns one part's arrays. A program takes and returns all parts, laid end to end along the dimension named above; an argument that names none is the same for every part. Nothing has to cross between parts.
Inputs may be any that keep to these rules, and one draw needn't show every extreme that they name: `lengths`: in each index of dp the counts sum to 176, and the largest of them is exactly 88.
All inputs are finite; a program needn't handle non-finite values.
Results may differ from the reference program's by a relative error of at most 0.0057.
Values may be sent and summed in bfloat16 or wider, within the bound.
No kernel may reach another device: no remote copies, remote signals or barrier semaphores. Data moves between devices by JAX's collectives and lax.ppermute only.
A program may use at most 128 MiB of HBM per device.

```python
import math
import jax
import jax.numpy as jnp
import numpy as np
from jax import lax

DM = 4096
FF = 14336
RANK = 32
QN = 8
TOK_DEV = 176
DOCS = 4
SEQMAX = 88
QR = 256
TOKENS = 1408
N_DP = 8
N_FAC = 2


def block_scale(own_key, dims, split, smallest, largest):
    gain = 1.0
    for axis_at, parts in split:
        draws = jax.random.uniform(jax.random.fold_in(jax.random.fold_in(own_key, 6), axis_at), (parts,), jnp.float32, smallest / len(split), largest / len(split))
        gain = gain * jnp.repeat(jnp.exp(draws), dims[axis_at] // parts).reshape((-1,) + (1,) * (len(dims) - 1 - axis_at))
    return gain


def length_profile(amount, total, limit, skew):
    portions = [(1 << 20) // math.isqrt(rank ** skew) + 1 for rank in range(2, amount + 1)]
    spare, holding = total - limit - (amount - 1), [1] * (amount - 1)
    while spare > 0:
        movable = [i for i in range(amount - 1) if holding[i] < limit]
        mass, left = sum([portions[i] for i in movable]), spare
        for i in movable:
            more = min(limit - holding[i], max(1, left * portions[i] // mass), spare)
            holding[i] = holding[i] + more
            spare = spare - more
    return np.array([limit] + holding)


def uneven_parts(rng, amount, total, reach, lean):
    if amount == 2:
        one = jax.random.randint(rng, (), max(1, total - reach), min(reach, total - 1) + 1)
        return jnp.stack([one, total - one])
    tallies = jnp.asarray(length_profile(amount, total, reach, lean), jnp.int32)
    pairs = (amount - 1) // 2
    giver, receiver = tallies[1:1 + 2 * pairs:2], tallies[2:2 + 2 * pairs:2]
    room = jnp.minimum(giver - 1, reach - receiver)
    shifted = jax.random.randint(jax.random.fold_in(rng, 1), (pairs,), 0, 1 << 20) % (room + 1)
    tallies = tallies.at[1:1 + 2 * pairs:2].set(giver - shifted).at[2:2 + 2 * pairs:2].set(receiver + shifted)
    return tallies[jax.random.permutation(jax.random.fold_in(rng, 2), amount)]


def normal_values(stream_key, shape, deviation, reach, cuts=(), held_as=jnp.bfloat16):
    factor_of = block_scale(stream_key, shape, cuts, -0.22, 0.18) if cuts else 1.0
    drawn = jax.random.normal(stream_key, shape, jnp.float32) * deviation * factor_of
    return jnp.minimum(jnp.maximum(drawn, -reach), reach).astype(held_as)


def setup_inputs(seed: int = 0, part: int = 0) -> dict:
    key_list = jax.random.split(jax.random.key(seed), 10)
    part_keys = jax.random.split(jax.random.fold_in(key_list[9], part), 10)
    return {
        "acts": normal_values(part_keys[0], (TOKENS, FF), 1.0, 6.0, ((0, 8), (1, 2))),
        "grads": normal_values(part_keys[1], (TOKENS, DM), 1.0, 6.0, ((0, 8), (1, 2))),
        "lengths": jax.vmap(lambda own: uneven_parts(own, DOCS, TOK_DEV, SEQMAX, 1))(jax.random.split(part_keys[2], N_DP)).reshape((N_DP, DOCS)).astype(jnp.int32),
        "basis_a": normal_values(key_list[3], (N_FAC, FF // N_FAC, FF), FF ** -0.5, 0.046875, ((0, 2), (1, 8))),
        "basis_g": normal_values(key_list[4], (N_FAC, DM // N_FAC, DM), DM ** -0.5, 0.09375, ((0, 2), (1, 8))),
        "coef_a": normal_values(key_list[5], (FF, QR), (25 * FF) ** -0.5, 0.009765625, ((0, 16),)),
        "coef_g": normal_values(key_list[6], (DM, QR), (25 * DM) ** -0.5, 0.01953125, ((0, 16),)),
        "eig_a": jnp.clip(jnp.exp(math.log(2.0) - 4.6051702 * jax.random.uniform(key_list[7], (FF,), jnp.float32) ** block_scale(key_list[7], (FF,), ((0, 16),), -0.2, 0.2)), 0.02, 2.0),
        "eig_g": jnp.clip(jnp.exp(math.log(2.0) - 4.6051702 * jax.random.uniform(key_list[8], (DM,), jnp.float32) ** block_scale(key_list[8], (DM,), ((0, 16),), -0.2, 0.2)), 0.02, 2.0),
    }


damping = 0.1

def reference(acts, grads, lengths, basis_a, basis_g, coef_a, coef_g, eig_a, eig_g):
    scaled_a = (coef_a.astype(jnp.float32) / (eig_a[:, None] + damping)).astype(jnp.bfloat16)
    scaled_g = (coef_g.astype(jnp.float32) / (eig_g[:, None] + damping)).astype(jnp.bfloat16)
    factor_a = jnp.dot(basis_a.reshape(FF, FF), scaled_a, preferred_element_type=jnp.float32).astype(jnp.bfloat16)
    factor_g = jnp.dot(basis_g.reshape(DM, DM), scaled_g, preferred_element_type=jnp.float32).astype(jnp.bfloat16)
    proj_a = jnp.dot(acts, factor_a, preferred_element_type=jnp.float32)
    proj_g = jnp.dot(grads, factor_g, preferred_element_type=jnp.float32)
    products = (proj_a * proj_g).reshape(N_DP, TOK_DEV, QN, RANK).sum(axis=3)
    doc_ends = jnp.cumsum(lengths, axis=1).astype(jnp.int32)
    doc_starts = (doc_ends - lengths).astype(jnp.int32)
    position = jnp.arange(TOK_DEV, dtype=jnp.int32)
    member = ((position[None, :, None] >= doc_starts[:, None, :]) & (position[None, :, None] < doc_ends[:, None, :])).astype(jnp.float32)
    sums = jnp.einsum('ntd,ntq->ndq', member, products, precision=lax.Precision.HIGHEST)
    divisor = jnp.sqrt(RANK * lengths.astype(jnp.float32))
    return (sums / divisor[:, :, None]).reshape(N_DP * DOCS, QN)
```

```python
import functools

import jax
import jax.numpy as jnp
import numpy as np
from jax import lax
from jax.experimental import pallas as pl
from jax.experimental.pallas import tpu as pltpu
from jax.sharding import PartitionSpec as P

RANK = 32
LANES = 128
MAX_RING = 16

damping = 0.1


AXES = ("parts", "dp", "fac")


def gathered(acts, grads, lengths, basis_a, basis_g, coef_a, coef_g, eig_a, eig_g):
    scaled_a = (coef_a.astype(jnp.float32) / (eig_a[:, None] + damping)).astype(jnp.bfloat16)
    scaled_g = (coef_g.astype(jnp.float32) / (eig_g[:, None] + damping)).astype(jnp.bfloat16)
    query_cols = scaled_a.shape[1]
    coef_rows_a = scaled_a.shape[0]
    coef_rows = coef_rows_a + scaled_g.shape[0]
    coef_stack = jnp.concatenate([scaled_a, scaled_g], axis=0)
    section = lax.all_gather(coef_stack, ("dp", "fac"), axis=0, tiled=True)
    blocks = section.reshape(-1, coef_rows, query_cols)
    part_a = blocks[:, :coef_rows_a].reshape(-1, query_cols)
    part_g = blocks[:, coef_rows_a:].reshape(-1, query_cols)
    factor_a = jnp.dot(basis_a[0], part_a, preferred_element_type=jnp.float32).astype(jnp.bfloat16)
    factor_g = jnp.dot(basis_g[0], part_g, preferred_element_type=jnp.float32).astype(jnp.bfloat16)
    proj_a = jnp.dot(
        acts, lax.all_gather(factor_a, "dp", axis=0, tiled=True), preferred_element_type=jnp.float32
    )
    proj_g = jnp.dot(
        grads, lax.all_gather(factor_g, "dp", axis=0, tiled=True), preferred_element_type=jnp.float32
    )
    share_a = lax.psum_scatter(proj_a, "fac", scatter_dimension=1, tiled=True)
    share_g = lax.psum_scatter(proj_g, "fac", scatter_dimension=1, tiled=True)
    tok_rows = acts.shape[0]
    products = (share_a * share_g).reshape(tok_rows, -1, RANK).sum(axis=2)
    counts = lengths[0]
    doc_ends = jnp.cumsum(counts)
    doc_starts = doc_ends - counts
    position = jnp.arange(tok_rows, dtype=jnp.int32)
    member = (
        (position[:, None] >= doc_starts[None, :]) & (position[:, None] < doc_ends[None, :])
    ).astype(jnp.float32)
    sums = jnp.einsum("td,tq->dq", member, products, precision=lax.Precision.HIGHEST)
    return sums / jnp.sqrt(RANK * counts.astype(jnp.float32))[:, None]


def scale_kernel(part_ref, ca_ref, cg_ref, ea_ref, eg_ref, out_ref):
    base = 0
    for c_ref, e_ref in ((ca_ref, ea_ref), (cg_ref, eg_ref)):
        rows = c_ref.shape[0]
        for k in range(0, rows, LANES):
            eig = jnp.broadcast_to(e_ref[:, k : k + LANES] + damping, (LANES, LANES)).T
            out_ref[base + k : base + k + LANES, :] = (
                c_ref[k : k + LANES, :].astype(jnp.float32) / eig
            ).astype(out_ref.dtype)
        base += rows


def scale(part, coef_a, coef_g, eig_a, eig_g, half):
    ra, rg = coef_a.shape[0], coef_g.shape[0]
    return pl.pallas_call(
        scale_kernel,
        out_shape=jax.ShapeDtypeStruct((ra + rg, half), coef_a.dtype),
        grid_spec=pltpu.PrefetchScalarGridSpec(
            num_scalar_prefetch=1,
            grid=(1,),
            in_specs=[
                pl.BlockSpec((ra, half), lambda i, p: (0, p[0])),
                pl.BlockSpec((rg, half), lambda i, p: (0, p[0])),
                pl.BlockSpec((1, ra), lambda i, p: (0, 0)),
                pl.BlockSpec((1, rg), lambda i, p: (0, 0)),
            ],
            out_specs=pl.BlockSpec((ra + rg, half), lambda i, p: (0, 0)),
        ),
        name="scale",
    )(part, coef_a, coef_g, eig_a.reshape(1, ra), eig_g.reshape(1, rg))


def factor_kernel(nb, first, tile, ra, rg, *refs):
    refs = refs[1:]
    ba, bg, c = refs[:nb], refs[nb : 2 * nb], refs[2 * nb : 3 * nb]
    acc_ref = None if first else refs[3 * nb]
    out_ref = refs[-1]
    t = pl.program_id(0)
    rows = pl.ds(pl.multiple_of(t * tile, tile), tile)
    total = None if first else acc_ref[rows, :]
    for j in range(nb):
        term = jnp.dot(ba[j][...], c[j][:ra, :], preferred_element_type=jnp.float32)
        total = term if total is None else total + term
    out_ref[rows, :] = total.astype(out_ref.dtype)

    @pl.when(t == 0)
    def _():
        sums = None if first else acc_ref[ra:, :]
        for j in range(nb):
            term = jnp.dot(bg[j][...], c[j][ra:, :], preferred_element_type=jnp.float32)
            sums = term if sums is None else sums + term
        out_ref[ra:, :] = sums.astype(out_ref.dtype)


def factor_step(index, basis_a, basis_g, blocks, ra, rg, acc, out_dtype):
    nb = len(blocks)
    tiles = 4 if ra % 64 == 0 else 1
    tile = ra // tiles
    half = blocks[0].shape[1]
    whole = pl.BlockSpec((ra + rg, half), lambda t, i: (0, 0))
    first = acc is None
    ka = basis_a.shape[1] // (basis_a.shape[1] // ra)
    return pl.pallas_call(
        functools.partial(factor_kernel, nb, first, tile, ra, rg),
        out_shape=jax.ShapeDtypeStruct((ra + rg, half), out_dtype),
        grid_spec=pltpu.PrefetchScalarGridSpec(
            num_scalar_prefetch=1,
            grid=(tiles,),
            in_specs=[pl.BlockSpec((tile, ka), lambda t, i, j=j: (t, i[j])) for j in range(nb)]
            + [pl.BlockSpec((rg, rg), lambda t, i, j=j: (0, i[j])) for j in range(nb)]
            + [whole] * nb
            + ([] if first else [whole]),
            out_specs=whole,
        ),
        cost_estimate=pl.CostEstimate(
            flops=2 * nb * half * (ra * ra + rg * rg),
            bytes_accessed=2 * nb * (ra * ra + rg * rg),
            transcendentals=0,
        ),
        name="factor_step",
    )(index, *[basis_a] * nb, *[basis_g] * nb, *blocks, *([] if first else [acc]))


def proj_kernel(nb, first, last, ra, *refs):
    idx = refs[0]
    refs = refs[1:]
    xa, xg = refs[:nb], refs[nb : 2 * nb]
    s, o = refs[2 * nb : 3 * nb], refs[3 * nb : 4 * nb]
    accs = [None, None] if first else refs[4 * nb : 4 * nb + 2]
    out_p, out_o = refs[-2:]
    tok = xa[0].shape[0]
    results = []
    for blocks, acc in ((s, accs[0]), (o, accs[1])):
        ta = None if first else acc[:tok, :]
        tg = None if first else acc[tok:, :]
        for j in range(nb):
            da = jnp.dot(xa[j][...], blocks[j][:ra, :], preferred_element_type=jnp.float32)
            dg = jnp.dot(xg[j][...], blocks[j][ra:, :], preferred_element_type=jnp.float32)
            ta = da if ta is None else ta + da
            tg = dg if tg is None else tg + dg
        results.append((ta, tg))
    (pa, pg), (oa, og) = results
    if last:
        mine = idx[nb] == 1
        pa, oa = jnp.where(mine, pa, oa), jnp.where(mine, oa, pa)
        pg, og = jnp.where(mine, pg, og), jnp.where(mine, og, pg)
    out_p[:tok, :] = pa
    out_p[tok:, :] = pg
    out_o[:tok, :] = oa
    out_o[tok:, :] = og


def proj_step(index, xs, s, o, ra, rg, acc, last):
    nb = len(s)
    tok = xs[0][0].shape[0]
    half = s[0].shape[1]
    first = acc is None
    block = pl.BlockSpec((ra + rg, half), lambda t, i: (0, 0))
    total = pl.BlockSpec((2 * tok, half), lambda t, i: (0, 0))
    shape = jax.ShapeDtypeStruct((2 * tok, half), jnp.float32)
    return pl.pallas_call(
        functools.partial(proj_kernel, nb, first, last, ra),
        out_shape=(shape, shape),
        grid_spec=pltpu.PrefetchScalarGridSpec(
            num_scalar_prefetch=1,
            grid=(1,),
            in_specs=[pl.BlockSpec((tok, ra), lambda t, i, j=j: (0, i[j])) for j in range(nb)]
            + [pl.BlockSpec((tok, rg), lambda t, i, j=j: (0, i[j])) for j in range(nb)]
            + [block] * (2 * nb)
            + ([] if first else [total] * 2),
            out_specs=(total, total),
        ),
        cost_estimate=pl.CostEstimate(
            flops=4 * nb * half * tok * (ra + rg),
            bytes_accessed=2 * nb * (ra + rg) * (tok + 2 * half),
            transcendentals=0,
        ),
        name="proj_step",
    )(index, *[x[0] for x in xs], *[x[1] for x in xs], *s, *o, *([] if first else acc))


def score_kernel(docs, len_ref, mine_ref, came_ref, out_ref):
    tok = mine_ref.shape[0] // 2
    total = mine_ref[...] + came_ref[...]
    prod = total[:tok, :] * total[tok:, :]
    row = lax.broadcasted_iota(jnp.int32, prod.shape, 0)
    lane = lax.broadcasted_iota(jnp.int32, (1, prod.shape[1]), 1)
    queries = out_ref.shape[1]
    shape = out_ref.shape
    doc_at = lax.broadcasted_iota(jnp.int32, shape, 0)
    query_at = lax.broadcasted_iota(jnp.int32, shape, 1)
    out = jnp.zeros(shape, jnp.float32)
    start = jnp.int32(0)
    for d in range(docs):
        count = len_ref[0, d]
        end = start + count
        inside = (row >= start) & (row < end)
        per_lane = jnp.sum(jnp.where(inside, prod, 0.0), axis=0, keepdims=True)
        root = jnp.sqrt(jnp.full((1, 1), RANK, jnp.float32) * count.astype(jnp.float32))
        for q in range(queries):
            one = jnp.sum(
                jnp.where((lane >= q * RANK) & (lane < (q + 1) * RANK), per_lane, 0.0),
                axis=1,
                keepdims=True,
            )
            out = jnp.where((doc_at == d) & (query_at == q), one / root, out)
        start = end
    out_ref[...] = out


def score(lengths, mine, came, half):
    docs = lengths.shape[1]
    return pl.pallas_call(
        functools.partial(score_kernel, docs),
        out_shape=jax.ShapeDtypeStruct((docs, half // RANK), jnp.float32),
        in_specs=[
            pl.BlockSpec(memory_space=pltpu.SMEM),
            pl.BlockSpec(memory_space=pltpu.VMEM),
            pl.BlockSpec(memory_space=pltpu.VMEM),
        ],
        out_specs=pl.BlockSpec(memory_space=pltpu.VMEM),
        name="score",
    )(lengths, mine, came)


class Ring:
    def __init__(self, parts, n):
        self.parts, self.n, self.steps = parts, n, n // 2
        self.order = list(range(0, n, 2)) + list(range(n - 1, 0, -2))
        self.pos = {d: i for i, d in enumerate(self.order)}

    def item(self, d, f, s):
        move = -s if f == 0 else s
        return self.order[(self.pos[d] + move) % self.n]

    def pairs(self, where):
        out = []
        for p in range(self.parts):
            for d in range(self.n):
                for f in range(2):
                    q, e, g = where(p, d, f)
                    out.append(((p * self.n + d) * 2 + f, (q * self.n + e) * 2 + g))
        return out

    def onward(self):
        return self.pairs(
            lambda p, d, f: (p, self.order[(self.pos[d] + (1 if f == 0 else -1)) % self.n], f)
        )

    def other_core(self):
        return self.pairs(lambda p, d, f: (p, d, 1 - f))

    def other_part(self):
        return self.pairs(lambda p, d, f: (1 - p, d, f))


def ringed(parts, n, acts, grads, lengths, basis_a, basis_g, coef_a, coef_g, eig_a, eig_g):
    ring = Ring(parts, n)
    onward, other_core, other_part = ring.onward(), ring.other_core(), ring.other_part()
    go = lambda x: lax.ppermute(x, AXES, onward)
    core = lambda x: lax.ppermute(x, AXES, other_core)
    part = lambda x: lax.ppermute(x, AXES, other_part)
    steps = ring.steps
    ra, rg = coef_a.shape[0], coef_g.shape[0]
    half = coef_a.shape[1] // 2
    panel_a, panel_g = basis_a[0], basis_g[0]

    p, d, f = (lax.axis_index(a) for a in AXES)
    table = []
    for e in range(n):
        for g in range(2):
            row = [e * 2 + g, e * 2 + 1 - g]
            for s in range(1, steps):
                row += [ring.item(e, g, s) * 2 + g, ring.item(e, g, s) * 2 + 1 - g]
                row += [ring.item(e, 1 - g, s) * 2 + 1 - g, ring.item(e, 1 - g, s) * 2 + g]
            row += [ring.item(e, g, steps) * 2 + g, ring.item(e, 1 - g, steps) * 2 + 1 - g]
            row += [e] + [ring.item(e, g, s) for s in range(1, steps + 1)]
            table.append(row)
    table = jnp.asarray(np.array(table, np.int32))
    mine = lax.dynamic_slice_in_dim(table, d * 2 + f, 1, axis=0)[0]
    k_index = mine[: 4 * steps]
    dp_index = mine[4 * steps :]

    own = scale(p[None].astype(jnp.int32), coef_a, coef_g, eig_a, eig_g, half)
    partner_acts = None
    a, b = own, core(own)
    acc = factor_step(k_index[:2], panel_a, panel_g, [a, b], ra, rg, None, jnp.float32)
    for s in range(1, steps + 1):
        a = go(a)
        blocks = [a]
        if s < steps:
            b = go(b)
            blocks += [b]
        blocks += [core(x) for x in blocks]
        at = 2 + 4 * (s - 1)
        last = s == steps
        acc = factor_step(
            k_index[at : at + len(blocks)], panel_a, panel_g, blocks, ra, rg, acc,
            jnp.bfloat16 if last else jnp.float32,
        )
    factor = acc

    here = (acts, grads)
    there = (core(acts), core(grads))
    a, b = factor, core(factor)
    flag = (p == f).astype(jnp.int32)[None]
    groups = [([factor], [here], [0])]
    for s in range(1, steps + 1):
        a = go(a)
        if s < steps:
            b = go(b)
            groups.append(([a, b], [here, there], [s, s]))
        else:
            groups.append(([a], [here], [s]))
    sums = None
    for k, (blocks, xs, at) in enumerate(groups):
        others = [part(x) for x in blocks]
        index = jnp.concatenate([dp_index[i : i + 1] for i in at] + [flag])
        sums = proj_step(index, xs, blocks, others, ra, rg, sums, k == len(groups) - 1)
    kept, sent = sums
    return score(lengths, kept, core(sent), half)


def fits(mesh, coef_a, coef_g, acts):
    parts, n, fac = (mesh.shape[a] for a in AXES)
    shards = n * fac
    ra, rg = coef_a.shape[0] // shards, coef_g.shape[0] // shards
    half = coef_a.shape[1] // 2
    return (
        parts == 2
        and fac == 2
        and n % 2 == 0
        and n <= MAX_RING
        and ra % LANES == 0
        and rg % LANES == 0
        and half == LANES
        and half % RANK == 0
        and acts.shape[0] // (parts * n) % 8 == 0
    )


def solution(mesh):
    placed = (
        P(("parts", "dp"), "fac"),
        P(("parts", "dp"), "fac"),
        P(("parts", "dp"), None),
        P("fac", "dp", None),
        P("fac", "dp", None),
        P(("dp", "fac"), None),
        P(("dp", "fac"), None),
        P(("dp", "fac")),
        P(("dp", "fac")),
    )

    def program(acts, grads, lengths, basis_a, basis_g, coef_a, coef_g, eig_a, eig_g):
        if fits(mesh, coef_a, coef_g, acts):
            body = functools.partial(ringed, mesh.shape["parts"], mesh.shape["dp"])
        else:
            body = gathered
        return jax.shard_map(
            body, mesh=mesh, in_specs=placed, out_specs=P(("parts", "dp"), "fac"), check_vma=False
        )(acts, grads, lengths, basis_a, basis_g, coef_a, coef_g, eig_a, eig_g)

    return program
```
